512 devices in a mesh: ket: 128 (over z, y, core), blk: 4 (over x).
Axes of the slice: x: 4, y: 8, z: 8, core: 2. Of those that a mesh axis runs over, the one named last changes fastest.
Arguments:
- density: float32 [8192, 64, 128], P('ket', 'blk'), may hold values from -24 to 24
- decay_matrix: float32 [128, 128], replicated, may hold values from -0.25 to 2, as said below
- atom_order: int32 [128], replicated, may hold values from 0 to 127, each once
Outputs:
- next_vector: float32 [8192, 64, 128], P('ket', 'blk')
- krylov_coeffs: float32 [5], replicated
- jump_flux: float32 [8192], P(('ket', 'blk'))
The draws below stay inside these ranges and needn't reach their ends.
Inputs may be any that keep to these rules, and one draw needn't show every extreme that they name: `decay_matrix`: symmetric; diagonal entries from 0.5 to 2, off-diagonal entries at most 0.25 in magnitude. `atom_order`: each atom once.
All inputs are finite; a program needn't handle non-finite values.
Results may differ from the reference program's by a relative error of at most 0.0003.
Values sent between devices are 32-bit elements; how exact they have to be, the bound alone decides.
No kernel may reach another device: no remote copies, remote signals or barrier semaphores. Data moves between devices by JAX's collectives and lax.ppermute only.
A program may use at most 64 MiB of HBM per device.

```python
import math
import jax
import jax.numpy as jnp
from jax import lax

N = 128
H = 64
P_SIZE = 8192


def draw_decay_matrix(key, part):
    base = jax.random.fold_in(key, 11)
    first_key, second_key = jax.random.split(base)
    diagonal = jnp.exp(jax.random.uniform(first_key, (N,), jnp.float32, math.log(0.5), math.log(2.0)))
    spread = 0.35
    diagonal = jnp.clip(diagonal, 0.5, 2.0)
    normals = jax.random.normal(second_key, (N, N), jnp.float32)
    offdiag = jnp.clip((normals + normals.T) * (spread / math.sqrt(N)), -0.25, 0.25)
    identity = jnp.arange(N)[:, None] == jnp.arange(N)[None, :]
    return jnp.where(identity, diagonal[:, None], offdiag).astype(jnp.float32)


def strengthened(values, rng, source, target, parts, factor):
    def block_of(axis_at):
        return (jnp.arange(values.shape[axis_at]) // (values.shape[axis_at] // parts)).reshape((-1,) + (1,) * (values.ndim - 1 - axis_at))

    one_side = jax.random.permutation(rng, parts)[block_of(target)]
    second = (block_of(target) + parts // 2) % parts
    return jnp.where((block_of(source) == one_side) | (block_of(source) == second), factor * values, values)


def level_of(rng, shape, cuts, smallest, high):
    loudness, own = 1.0, jax.random.fold_in(rng, 6)
    for dim, shards_of in cuts:
        heights = jnp.exp(jax.random.uniform(jax.random.fold_in(own, dim), (shards_of,), jnp.float32, smallest / len(cuts), high / len(cuts)))
        loudness = loudness * jnp.repeat(heights, shape[dim] // shards_of).reshape([-1 if axis == dim else 1 for axis in range(len(shape))])
    return loudness


def noise_with(own_key, dims, width, bound, pieces, heavy, kind=jnp.bfloat16):
    values = width * jax.random.normal(own_key, dims, jnp.float32)
    if pieces:
        values = values * level_of(own_key, dims, pieces, -0.22, 0.18)
    return jnp.clip(strengthened(values, jax.random.fold_in(own_key, 3), *heavy), -bound, bound).astype(kind)


def setup_inputs(seed: int = 0) -> dict:
    arg_keys = jax.random.split(jax.random.key(seed), 4)
    return {
        "density": noise_with(arg_keys[0], (P_SIZE, H, N), 1.0, 24.0, ((0, 128), (1, 4)), (0, 2, 128, 5.5), jnp.float32),
        "decay_matrix": draw_decay_matrix(jax.random.fold_in(arg_keys[3], 71), 0),
        "atom_order": jax.random.permutation(arg_keys[2], N).astype(jnp.int32),
    }


highest = lax.Precision.HIGHEST

def liouvillian(tensor, coupling):
    atom_count = coupling.shape[0]
    half = tensor.shape[1]
    window = coupling[:half, :half]
    leading = jnp.dot(coupling, tensor.reshape(atom_count, -1), precision=highest).reshape(tensor.shape)
    ket_slabs = tensor.reshape(atom_count, half, half, atom_count)

    def slab_terms(ket_slab):
        return jnp.einsum('jb,bkl->jkl', window, ket_slab, precision=highest) + jnp.einsum('kc,jcl->jkl', window, ket_slab, precision=highest) + jnp.einsum('ld,jkd->jkl', coupling, ket_slab, precision=highest)
    others = lax.map(slab_terms, ket_slabs).reshape(tensor.shape)
    return -0.5 * (leading + others)

def krylov_step(vectors, image_vec, entries):
    correlation = jnp.stack([jnp.sum(vector * image_vec) for vector in vectors]) / entries
    residual = image_vec
    for position in range(len(vectors)):
        residual = residual - correlation[position] * vectors[position]
    length_value = jnp.sqrt(jnp.sum(residual * residual) / entries)
    return (correlation, length_value, residual / length_value)

def reference(density, decay_matrix, atom_order):
    coupling = decay_matrix[atom_order][:, atom_order]
    atom_count = coupling.shape[0]
    half = density.shape[1]
    entries = float(density.size)
    vector_one = density / jnp.sqrt(jnp.sum(density * density) / entries)
    coeff_one, length_one, vector_two = krylov_step([vector_one], liouvillian(vector_one, coupling), entries)
    coeff_two, length_two, next_vector = krylov_step([vector_one, vector_two], liouvillian(vector_two, coupling), entries)
    krylov_coeffs = jnp.concatenate([coeff_one, length_one[None], coeff_two, length_two[None]])
    jump_flux = jnp.einsum('ab,ajbl->jl', coupling[:, :half], density.reshape(atom_count, half, half, atom_count), precision=highest).reshape(-1) / atom_count
    return (next_vector, krylov_coeffs, jump_flux)
```

```python
import jax
import jax.numpy as jnp
from jax import lax
from jax.experimental import pallas as pl
from jax.experimental.pallas import tpu as pltpu
from jax.sharding import PartitionSpec as P


AXES = ("ket", "blk")
LANES = 128
HIGHEST = lax.Precision.HIGHEST
F32 = jnp.float32


def dot(a, b):
    return jnp.dot(a, b, precision=HIGHEST, preferred_element_type=F32)


def iota(shape, axis):
    return lax.broadcasted_iota(jnp.int32, shape, axis)


def vmem_call(body, shapes, name, n_vmem, n_smem=0, scratch=()):
    in_specs = [pl.BlockSpec(memory_space=pltpu.SMEM)] * n_smem
    in_specs += [pl.BlockSpec(memory_space=pltpu.VMEM)] * n_vmem
    return pl.pallas_call(
        body,
        out_shape=[jax.ShapeDtypeStruct(shape, F32) for shape in shapes],
        in_specs=in_specs,
        out_specs=[pl.BlockSpec(memory_space=pltpu.VMEM)] * len(shapes),
        scratch_shapes=list(scratch),
        name=name,
    )


def send_body(x_ref, out_ref):
    for c in range(8):
        out_ref[pl.ds(c, 128, stride=8), :] = x_ref[c * 128:(c + 1) * 128, :].T


def apply_d(x_ref, shifted, window, wide_ref, out_ref):
    for k in range(16):
        wide_ref[:, k * 128:(k + 1) * 128] = x_ref[pl.ds(k, 64, stride=16), :]
    wide_ref[...] = dot(window, wide_ref[...])
    for k in range(16):
        out_ref[pl.ds(k, 64, stride=16), :] = wide_ref[:, k * 128:(k + 1) * 128]
    out_ref[...] += dot(x_ref[...], shifted)


def prep_body(x_ref, decay_ref, order_ref, dx_ref, g_ref, shifted_ref, kron_ref, tau_ref, wide_ref):
    onehot = (order_ref[...] == iota((128, 128), 1)).astype(F32)
    g = dot(dot(onehot, decay_ref[...]), onehot.T)
    g_ref[...] = g
    rows, cols = iota((128, 128), 0), iota((128, 128), 1)
    weight = jnp.where(rows < 64, 2.0 / 128 + 2.0 / 64, 2.0 / 128)
    tau = jnp.sum(jnp.where(rows == cols, g * weight, 0.0), keepdims=True)
    tau_ref[...] = jnp.broadcast_to(tau, (8, 128))
    shifted = jnp.where(rows == cols, g - tau, g)
    shifted_ref[...] = shifted
    window = g[:64, :64]
    r512, c64 = iota((512, 64), 0), iota((512, 64), 1)
    spread = (c64 == (r512 // 128) * 16 + r512 % 16).astype(F32)
    full = dot(dot(spread, window), spread.T)
    r, c = iota((512, 512), 0), iota((512, 512), 1)
    kron_ref[...] = jnp.where((r // 16) % 8 == (c // 16) % 8, full, 0.0)
    apply_d(x_ref, shifted, window, wide_ref, dx_ref)


def turned_body(y_ref, g_ref, kron_ref, out_ref, jump_ref, cat_ref):
    g = g_ref[...]
    lane, col = iota((64, 128), 1), iota((64, 128), 0)
    jump = [jnp.zeros((1, 128), F32) for _ in range(2)]
    for kb in range(4):
        spread = (col == kb * 16 + lane % 16).astype(F32)
        weights = dot(g[:, :64], spread)
        for h in range(2):
            piece = y_ref[pl.ds(kb * 2 + h, 128, stride=8), :]
            cat_ref[h * 128:(h + 1) * 128, kb * 128:(kb + 1) * 128] = piece
            jump[h] += jnp.sum(weights * piece, axis=0, keepdims=True)
    jump_ref[...] = jnp.concatenate(jump + [jnp.zeros((6, 128), F32)], axis=0)

    def apply_c(cat):
        both = jnp.concatenate([dot(g, cat[:128]), dot(g, cat[128:])], axis=0)
        return both + dot(cat, kron_ref[...])

    for v in range(2):
        cat_ref[...] = apply_c(cat_ref[...])
        for kb in range(4):
            for h in range(2):
                out_ref[pl.ds(kb * 4 + v * 2 + h, 128, stride=16), :] = (
                    cat_ref[h * 128:(h + 1) * 128, kb * 128:(kb + 1) * 128]
                )


def moments_body(r_ref, x_ref, dx_ref, shifted_ref, g_ref, jump_ref, w_ref, z_ref, msg_ref, wide_ref, t_ref):
    for c in range(8):
        part = slice(c * 128, (c + 1) * 128)
        cx = r_ref[pl.ds((c // 2) * 4 + c % 2, 128, stride=16), :].T
        w_ref[part, :] = dx_ref[part, :] + cx
        t_ref[part, :] = dx_ref[part, :] + 2.0 * cx
    apply_d(t_ref, shifted_ref[...], g_ref[:64, :64], wide_ref, z_ref)
    for c in range(8):
        part = slice(c * 128, (c + 1) * 128)
        z_ref[part, :] += r_ref[pl.ds((c // 2) * 4 + 2 + c % 2, 128, stride=16), :].T
    x, w, z = x_ref[...], w_ref[...], z_ref[...]
    lane = iota((1, 128), 1)
    row = jnp.zeros((1, 128), F32)
    for slot, product in enumerate((x * x, x * w, w * w, w * z, z * z)):
        row = jnp.where(lane == slot, jnp.sum(product, keepdims=True), row)
    n, at = iota((512, 128), 0), iota((512, 128), 1)
    jump = jnp.where((n // 64) % 2 == 0, jump_ref[0:1, :], jump_ref[1:2, :])
    picked = jnp.sum(jnp.where(at // 16 == (n // 8) % 8, jump, 0.0), axis=1, keepdims=True)
    msg_ref[...] = jnp.where(at == 5, picked * (1.0 / 128), jnp.broadcast_to(row, (512, 128)))


def finish_body(me_ref, msg_ref, x_ref, w_ref, z_ref, tau_ref, out_ref, coeff_ref, jump_ref):
    msg = msg_ref[...]
    total = jnp.sum(msg, axis=0, keepdims=True)
    lane = iota((1, 128), 1)

    def pick(slot):
        return jnp.sum(jnp.where(lane == slot, total, 0.0), keepdims=True)

    m0, m1, m2, m3, m4 = (pick(slot) for slot in range(5))
    m1, m2, m3, m4 = m1 / m0, m2 / m0, m3 / m0, m4 / m0
    tau = tau_ref[0:1, 0:1]
    beta1_sq = m2 - m1 * m1
    beta1 = jnp.sqrt(beta1_sq)
    alpha1 = (m3 - 2.0 * m1 * m2 + m1 * m1 * m1) / beta1_sq
    norm_sq = (m4 - 2.0 * m1 * m3 + m1 * m1 * m2) / beta1_sq
    beta2 = jnp.sqrt(norm_sq - beta1_sq - alpha1 * alpha1)
    scale = lax.rsqrt(m0 * (1.0 / 67108864.0)) / (beta1 * beta2)
    on_x = (alpha1 * m1 - beta1_sq) * scale
    on_w = (m1 + alpha1) * scale
    out_ref[...] = z_ref[...] * scale - w_ref[...] * on_w + x_ref[...] * on_x
    values = (-0.5 * (m1 + tau), 0.5 * beta1, 0.5 * beta1, -0.5 * (alpha1 + tau), 0.5 * beta2)
    row = jnp.zeros((1, 128), F32)
    for slot, value in enumerate(values):
        row = jnp.where(lane == slot, value, row)
    coeff_ref[...] = jnp.broadcast_to(row, (8, 128))
    me = me_ref[0]
    s, t = iota((512, 128), 0), iota((512, 128), 1)
    source = ((me % 8) * 16 + t) * 4 + me // 128
    mine = jnp.sum(jnp.where(t == 5, msg, 0.0), axis=1, keepdims=True)
    found = jnp.sum(jnp.where(s == source, mine, 0.0), axis=0, keepdims=True)
    jump_ref[...] = jnp.broadcast_to(found, (8, 128))


def shards(density, decay_matrix, atom_order):
    x = density.reshape(1024, 128)
    wide = pltpu.VMEM((64, 2048), F32)

    def exchange(rows):
        return lax.all_to_all(rows, AXES, split_axis=0, concat_axis=0, tiled=True)

    (sent,) = vmem_call(send_body, [(1024, 128)], "send", 1)(x)
    turned = exchange(sent)
    dx, g, shifted, kron, tau = vmem_call(
        prep_body,
        [(1024, 128), (128, 128), (128, 128), (512, 512), (8, 128)],
        "prep", 3, scratch=[wide],
    )(x, decay_matrix, atom_order.reshape(128, 1))
    images, jump_row = vmem_call(
        turned_body, [(2048, 128), (8, 128)], "turned", 3,
        scratch=[pltpu.VMEM((256, 512), F32)],
    )(turned, g, kron)
    returned = exchange(images)
    w, z, message = vmem_call(
        moments_body, [(1024, 128), (1024, 128), (512, 128)], "moments", 6,
        scratch=[wide, pltpu.VMEM((1024, 128), F32)],
    )(returned, x, dx, shifted, g, jump_row)
    received = exchange(message)
    me = lax.axis_index("ket") * 4 + lax.axis_index("blk")
    out, coeffs, jump = vmem_call(
        finish_body, [(1024, 128), (8, 128), (8, 128)], "finish", 5, n_smem=1
    )(me.astype(jnp.int32).reshape(1), received, x, w, z, tau)
    return out.reshape(density.shape), coeffs[0, :5], jump[0, :16]


def solution(mesh):
    return jax.shard_map(
        shards,
        mesh=mesh,
        in_specs=(P("ket", "blk", None), P(), P()),
        out_specs=(P("ket", "blk", None), P(), P(("ket", "blk"))),
        check_vma=False,
    )
```
